512 devices in a mesh: freq: 32 (over z, x_lo, core), tm: 16 (over x_hi, y).
Axes of the slice: x: 4 (x_hi: 2, x_lo: 2; x = x_hi * 2 + x_lo), y: 8, z: 8, core: 2. Of those that a mesh axis runs over, the one named last changes fastest.
Arguments:
- observed: bfloat16 [32, 16, 2, 512, 512], P('freq', 'tm'), may hold values from -6 to 6
- source_beams: bfloat16 [32, 16, 2, 256, 512], P('freq', 'tm'), may hold values from -1.1953125 to 1.1953125
- source_order: int32 [256], replicated, may hold values from 0 to 255, each once
- initial_gains: float32 [32, 2, 32, 512], P('freq'), may hold values from -2 to 2, as said below
- blending: float32 [32, 32], replicated, may hold values from 0 to 1, as said below
Outputs:
- residual: bfloat16 [32, 16, 2, 512, 512], P('freq', 'tm')
- smoothed_gains: float32 [32, 2, 32, 512], P('freq', None, 'tm')
The draws below stay inside these ranges and needn't reach their ends.
Inputs may be any that keep to these rules, and one draw needn't show every extreme that they name: source_order holds every number of 0 to 255 once. Every row of blending is positive and sums to one. `initial_gains`: every complex gain has a magnitude between 0.5 and 2.
All inputs are finite; a program needn't handle non-finite values.
Results may differ from the reference program's by a relative error of at most 0.0034.
Values sent between devices are 32-bit elements; how exact they have to be, the bound alone decides.
No kernel may reach another device: no remote copies, remote signals or barrier semaphores. Data moves between devices by JAX's collectives and lax.ppermute only.
A program may use at most 64 MiB of HBM per device.

```python
import math
import jax
import jax.numpy as jnp
from jax import lax

S = 512
K = 32
P_SIZE = 8
NSRC = 256
NF = 32
NT = 16


def draw_initial_gains(key, part):
    level_key, angle_key = jax.random.split(jax.random.fold_in(key, 11))
    magnitude = jnp.exp(jax.random.uniform(level_key, (NF, K, S), jnp.float32, math.log(0.5), math.log(2.0)))
    angles = jax.random.uniform(angle_key, (NF, K, S), jnp.float32, -math.pi, math.pi)
    return jnp.stack([magnitude * jnp.cos(angles), magnitude * jnp.sin(angles)], axis=1)


def draw_blending(key, part):
    band_index = jnp.arange(NF)
    distance = jnp.abs(band_index[:, None] - band_index[None, :]).astype(jnp.float32)
    jitter = jax.random.uniform(jax.random.fold_in(key, 23), (NF, NF), jnp.float32, 0.5, 1.5)
    unscaled = jnp.exp(-distance * 4.0 / NF) * jitter
    return unscaled / jnp.sum(unscaled, axis=1, keepdims=True)


def shard_levels(own_key, shape, cuts, low, largest):
    factor_of, own = 1.0, jax.random.fold_in(own_key, 6)
    for axis_at, parts in cuts:
        steps = jnp.exp(jax.random.uniform(jax.random.fold_in(own, axis_at), (parts,), jnp.float32, low / len(cuts), largest / len(cuts)))
        factor_of = factor_of * jnp.repeat(steps, shape[axis_at] // parts).reshape([-1 if axis == axis_at else 1 for axis in range(len(shape))])
    return factor_of


def gaussian(own_key, extent, width, reach, shards=(), kind=jnp.bfloat16):
    entries = width * jax.random.normal(own_key, extent, jnp.float32)
    if shards:
        entries = entries * shard_levels(own_key, extent, shards, -0.22, 0.18)
    return jnp.clip(entries, -reach, reach).astype(kind)


def setup_inputs(seed: int = 0) -> dict:
    seeds = jax.random.split(jax.random.key(seed), 6)
    observed = gaussian(seeds[0], (NF, NT, 2, S, S), 1.0, 6.0, ((0, 32), (1, 16)))
    source_beams = gaussian(seeds[1], (NF, NT, 2, NSRC, S), 0.2, 1.1953125, ((0, 32), (1, 16)))
    source_order = jax.random.permutation(seeds[2], NSRC).astype(jnp.int32)
    initial_gains = draw_initial_gains(jax.random.fold_in(seeds[5], 71), 0)
    blending = draw_blending(jax.random.fold_in(seeds[5], 71), 0)
    return dict(observed=observed, source_beams=source_beams, source_order=source_order, initial_gains=initial_gains, blending=blending)


def beam_terms(beam_block, source_order):
    picked = jnp.take(beam_block, source_order, axis=1)
    return picked.reshape(2, K, P_SIZE, S).astype(jnp.float32)


def seeded_terms(gains, beams):
    real_part = gains[0][:, None, :] * beams[0] - gains[1][:, None, :] * beams[1]
    imag_part = gains[0][:, None, :] * beams[1] + gains[1][:, None, :] * beams[0]
    rounded = jnp.stack([real_part, imag_part]).astype(jnp.bfloat16)
    rounded = lax.optimization_barrier(rounded)
    return rounded.astype(jnp.float32)


def predict(seeded):
    flat = seeded.reshape(2, K * P_SIZE, S)
    real_part = jnp.einsum('cjp,cjq->pq', flat, flat)
    imag_part = jnp.einsum('jp,jq->pq', flat[1], flat[0]) - jnp.einsum('jp,jq->pq', flat[0], flat[1])
    return jnp.stack([real_part, imag_part])


def local_terms(observed_block, beam_block, gains, source_order):
    beams = beam_terms(beam_block, source_order)
    seeded = seeded_terms(gains, beams)
    model = predict(seeded)
    misfit = (observed_block.astype(jnp.float32) - model).astype(jnp.bfloat16)
    misfit = lax.optimization_barrier(misfit).astype(jnp.float32)
    flat = seeded.reshape(2, K * P_SIZE, S)
    prod_real = jnp.einsum('jq,pq->jp', flat[0], misfit[0]) - jnp.einsum('jq,pq->jp', flat[1], misfit[1])
    prod_imag = jnp.einsum('jq,pq->jp', flat[1], misfit[0]) + jnp.einsum('jq,pq->jp', flat[0], misfit[1])
    prod_real = prod_real.reshape(K, P_SIZE, S)
    prod_imag = prod_imag.reshape(K, P_SIZE, S)
    pull_real = jnp.sum(beams[0] * prod_real + beams[1] * prod_imag, axis=1)
    pull_imag = jnp.sum(beams[0] * prod_imag - beams[1] * prod_real, axis=1)
    highest = lax.Precision.HIGHEST
    gram_real = jnp.einsum('kjq,kiq->kji', seeded[0], seeded[0], precision=highest) + jnp.einsum('kjq,kiq->kji', seeded[1], seeded[1], precision=highest)
    gram_imag = jnp.einsum('kjq,kiq->kji', seeded[0], seeded[1], precision=highest) - jnp.einsum('kjq,kiq->kji', seeded[1], seeded[0], precision=highest)
    inner_real = jnp.einsum('kji,kip->kjp', gram_real, beams[0], precision=highest) + jnp.einsum('kji,kip->kjp', gram_imag, beams[1], precision=highest)
    inner_imag = jnp.einsum('kji,kip->kjp', gram_imag, beams[0], precision=highest) - jnp.einsum('kji,kip->kjp', gram_real, beams[1], precision=highest)
    denominator = jnp.sum(beams[0] * inner_real - beams[1] * inner_imag, axis=1)
    pull_real = pull_real + gains[0] * denominator
    pull_imag = pull_imag + gains[1] * denominator
    return jnp.stack([pull_real, pull_imag, denominator], axis=1)


def peel_block(observed_block, beam_block, gains, source_order):
    beams = beam_terms(beam_block, source_order)
    final = seeded_terms(gains, beams)
    return (observed_block.astype(jnp.float32) - predict(final)).astype(jnp.bfloat16)


def reference(observed, source_beams, source_order, initial_gains, blending):
    def band_terms(band_inputs):
        band_observed, band_beams, band_gains = band_inputs

        def time_terms(time_inputs):
            return local_terms(time_inputs[0], time_inputs[1], band_gains, source_order)

        return jnp.sum(lax.map(time_terms, (band_observed, band_beams)), axis=0)

    totals = lax.map(band_terms, (observed, source_beams, initial_gains))
    denominator = totals[:, :, 2]
    ratio = jnp.stack([totals[:, :, 0], totals[:, :, 1]], axis=1) / denominator[:, None]
    damped = 0.5 * (ratio + initial_gains)
    smoothed = jnp.einsum('fg,gcks->fcks', blending, damped, precision=lax.Precision.HIGHEST)

    def band_peel(band_inputs):
        band_observed, band_beams, band_gains = band_inputs

        def time_peel(time_inputs):
            return peel_block(time_inputs[0], time_inputs[1], band_gains, source_order)

        return lax.map(time_peel, (band_observed, band_beams))

    residual = lax.map(band_peel, (observed, source_beams, smoothed))
    return residual, smoothed
```

```python
import jax
import jax.numpy as jnp
from jax import lax
from jax.experimental import pallas as pl
from jax.experimental.pallas import tpu as pltpu
from jax.sharding import PartitionSpec as P

S = 512
K = 32
P_SIZE = 8
N = K * P_SIZE
HALF = 128
LANES = 128
NT_DIMS = (((1,), (1,)), ((), ()))
NN_DIMS = (((1,), (0,)), ((), ()))
TN_DIMS = (((0,), (0,)), ((), ()))
F32 = jnp.float32
BF16 = jnp.bfloat16


def dot(left, right, dims):
    return lax.dot_general(left, right, dims, preferred_element_type=F32)


def expand(rows):
    return jnp.concatenate(
        [jnp.broadcast_to(rows[k : k + 1], (P_SIZE, rows.shape[1])) for k in range(rows.shape[0])],
        axis=0,
    )


def rotated_pair(real, imag, gains_real, gains_imag):
    return (
        (gains_real * real - gains_imag * imag).astype(BF16),
        (gains_real * imag + gains_imag * real).astype(BF16),
    )


def direction_sums(values):
    return jnp.sum(values.reshape(values.shape[0] // P_SIZE, P_SIZE, values.shape[1]), axis=1)


def terms_kernel(observed, catalogue, order, gains, sums, beams, joined, turned):
    source = lax.broadcasted_iota(jnp.int32, (N, N), 0)
    pick = jnp.where(source == order[...], 1.0, 0.0).astype(BF16)
    for part in range(2):
        beams[part] = dot(pick, catalogue[part], TN_DIMS).astype(BF16)
    for half in range(2):
        rows = pl.ds(half * HALF, HALF)
        ks = pl.ds(half * (K // 2), K // 2)
        seeded_real, seeded_imag = rotated_pair(
            beams[0, rows, :].astype(F32),
            beams[1, rows, :].astype(F32),
            expand(gains[0, ks, :]),
            expand(gains[1, ks, :]),
        )
        base = half * 2 * HALF
        joined[pl.ds(base, HALF), :] = seeded_real
        joined[pl.ds(base + HALF, HALF), :] = seeded_imag
        turned[pl.ds(base, HALF), :] = seeded_imag
        turned[pl.ds(base + HALF, HALF), :] = -seeded_real
    row_dir = lax.broadcasted_iota(jnp.int32, (HALF, HALF), 0) // P_SIZE
    col_dir = lax.broadcasted_iota(jnp.int32, (HALF, HALF), 1) // P_SIZE
    same = row_dir == col_dir
    weights = []
    for half in range(2):
        rows = pl.ds(half * HALF, HALF)
        block = joined[pl.ds(half * 2 * HALF, 2 * HALF), :]
        grid = dot(block, block, NT_DIMS)
        gram_real = jnp.where(same, grid[:HALF, :HALF] + grid[HALF:, HALF:], 0.0)
        gram_imag = jnp.where(same, grid[:HALF, HALF:] - grid[HALF:, :HALF], 0.0)
        gram = jnp.concatenate(
            [
                jnp.concatenate([gram_real, gram_imag], axis=1),
                jnp.concatenate([gram_imag, -gram_real], axis=1),
            ],
            axis=0,
        )
        high = gram.astype(BF16)
        low = (gram - high.astype(F32)).astype(BF16)
        both = jnp.concatenate([beams[0, rows, :], beams[1, rows, :]], axis=0)
        inner = dot(high, both, NN_DIMS) + dot(low, both, NN_DIMS)
        real = beams[0, rows, :].astype(F32)
        imag = beams[1, rows, :].astype(F32)
        weights.append(direction_sums(real * inner[:HALF] - imag * inner[HALF:]))
    weight = jnp.concatenate(weights, axis=0)
    everything = joined[...]
    for chunk in range(2):
        cols = pl.ds(chunk * 256, 256)
        model_real = dot(joined[:, cols], everything, TN_DIMS)
        misfit_real = (observed[0, cols, :].astype(F32) - model_real).astype(BF16)
        model_imag = dot(turned[:, cols], everything, TN_DIMS)
        misfit_minus = (model_imag - observed[1, cols, :].astype(F32)).astype(BF16)
        product = dot(everything, misfit_real, NT_DIMS) + dot(turned[...], misfit_minus, NT_DIMS)
        pulls_real, pulls_imag = [], []
        for half in range(2):
            rows = pl.ds(half * HALF, HALF)
            base = half * 2 * HALF
            real = beams[0, rows, cols].astype(F32)
            imag = beams[1, rows, cols].astype(F32)
            product_real = product[base : base + HALF]
            product_imag = product[base + HALF : base + 2 * HALF]
            pulls_real.append(direction_sums(real * product_real + imag * product_imag))
            pulls_imag.append(direction_sums(real * product_imag - imag * product_real))
        weight_here = weight[:, chunk * 256 : chunk * 256 + 256]
        pull_real = jnp.concatenate(pulls_real, axis=0) + 2.0 * gains[0, :, cols] * weight_here
        pull_imag = jnp.concatenate(pulls_imag, axis=0) + 2.0 * gains[1, :, cols] * weight_here
        for group in range(4):
            for side in range(2):
                piece = group * 4 + chunk * 2 + side
                for part, value in enumerate((pull_real, pull_imag, weight_here)):
                    sums[piece, pl.ds(part * 8, 8), :] = value[
                        group * 8 : group * 8 + 8, side * LANES : (side + 1) * LANES
                    ]


def terms(observed, catalogue, order, gains):
    return pl.pallas_call(
        terms_kernel,
        out_shape=(
            jax.ShapeDtypeStruct((16, 24, LANES), F32),
            jax.ShapeDtypeStruct((2, N, S), BF16),
        ),
        scratch_shapes=[pltpu.VMEM((2 * N, S), BF16), pltpu.VMEM((2 * N, S), BF16)],
        cost_estimate=pl.CostEstimate(flops=2 * 10**9, bytes_accessed=2 * 10**6, transcendentals=0),
        name="terms",
    )(observed, catalogue, order, gains)


def peel_kernel(slot, observed, beams, smooth, residual, gains_out, joined, turned):
    for half in range(2):
        rows = pl.ds(half * HALF, HALF)
        base = half * 2 * HALF
        for block in range(4):
            lanes = pl.ds(block * LANES, LANES)
            gains = [
                jnp.concatenate(
                    [expand(smooth[part * 16 + group * 4 + block]) for group in (2 * half, 2 * half + 1)],
                    axis=0,
                )
                for part in range(2)
            ]
            final_real, final_imag = rotated_pair(
                beams[0, rows, lanes].astype(F32), beams[1, rows, lanes].astype(F32), *gains
            )
            joined[pl.ds(base, HALF), lanes] = final_real
            joined[pl.ds(base + HALF, HALF), lanes] = final_imag
            turned[pl.ds(base, HALF), lanes] = final_imag
            turned[pl.ds(base + HALF, HALF), lanes] = -final_real
    everything = joined[...]
    for chunk in range(2):
        cols = pl.ds(chunk * 256, 256)
        model_real = dot(joined[:, cols], everything, TN_DIMS)
        residual[0, cols, :] = (observed[0, cols, :].astype(F32) - model_real).astype(BF16)
        model_imag = dot(turned[:, cols], everything, TN_DIMS)
        residual[1, cols, :] = (observed[1, cols, :].astype(F32) - model_imag).astype(BF16)
    group = slot[0] // 4
    row = (slot[0] % 4) * 2
    for part in range(2):
        for block in range(4):
            gains_out[part, :, pl.ds(block * LANES, LANES)] = smooth[
                part * 16 + group * 4 + block, pl.ds(row, 2), :
            ]


def peel(slot, observed, beams, smooth):
    vmem = pl.BlockSpec(memory_space=pltpu.VMEM)
    return pl.pallas_call(
        peel_kernel,
        out_shape=(
            jax.ShapeDtypeStruct((2, S, S), BF16),
            jax.ShapeDtypeStruct((2, 2, S), F32),
        ),
        in_specs=[pl.BlockSpec(memory_space=pltpu.SMEM), vmem, vmem, vmem],
        scratch_shapes=[pltpu.VMEM((2 * N, S), BF16), pltpu.VMEM((2 * N, S), BF16)],
        cost_estimate=pl.CostEstimate(flops=10**9, bytes_accessed=3 * 10**6, transcendentals=0),
        name="peel",
    )(slot, observed, beams, smooth)


def local(observed, source_beams, source_order, initial_gains, blending):
    freqs, times = lax.axis_size("freq"), lax.axis_size("tm")
    observed_block = observed[0, 0]
    sums, beams = terms(
        observed_block, source_beams[0, 0], source_order.reshape(1, N), initial_gains[0]
    )
    pieces = lax.all_to_all(sums, "tm", split_axis=0, concat_axis=0, tiled=True)
    totals = jnp.sum(pieces, axis=0).reshape(3, 8, LANES)
    damped = 0.5 * (totals[:2] / totals[2])
    sent = jnp.broadcast_to(damped[None], (freqs // 2, 2, 8, LANES)).reshape(freqs, 8, LANES)
    bands = lax.all_to_all(sent, "freq", split_axis=0, concat_axis=0, tiled=True)
    first = (lax.axis_index("freq") // 2) * 2
    rows = lax.dynamic_slice_in_dim(blending, first, 2, 0)
    mixed = jnp.sum(rows[:, :, None, None] * bands[None], axis=1)
    spread = jnp.broadcast_to(mixed[:, None], (2, times, 8, LANES)).reshape(2 * times, 8, LANES)
    groups = [
        [(pair * 2 + core) * times + time for core in range(2) for time in range(times)]
        for pair in range(freqs // 2)
    ]
    smooth = lax.all_to_all(
        spread, ("freq", "tm"), split_axis=0, concat_axis=0, tiled=True, axis_index_groups=groups
    )
    slot = lax.axis_index("tm").reshape(1)
    residual, gains_out = peel(slot, observed_block, beams, smooth)
    return (residual[None, None], gains_out[None])


def solution(mesh):
    return jax.shard_map(
        local,
        mesh=mesh,
        in_specs=(
            P("freq", "tm", None, None, None),
            P("freq", "tm", None, None, None),
            P(),
            P("freq", None, None, None),
            P(),
        ),
        out_specs=(P("freq", "tm", None, None, None), P("freq", None, "tm", None)),
        check_vma=False,
    )
```

```python
import jax
import jax.numpy as jnp
from jax import lax
from jax.experimental import pallas as pl
from jax.experimental.pallas import tpu as pltpu
from jax.sharding import PartitionSpec as P

S = 512
K = 32
P_SIZE = 8
N = K * P_SIZE
HALF = 128
LANES = 128
NT_DIMS = (((1,), (1,)), ((), ()))
NN_DIMS = (((1,), (0,)), ((), ()))
TN_DIMS = (((0,), (0,)), ((), ()))
F32 = jnp.float32
BF16 = jnp.bfloat16


def dot(left, right, dims):
    return lax.dot_general(left, right, dims, preferred_element_type=F32)


def expand(rows):
    return jnp.concatenate(
        [jnp.broadcast_to(rows[k : k + 1], (P_SIZE, rows.shape[1])) for k in range(rows.shape[0])],
        axis=0,
    )


def rotated_pair(real, imag, gains_real, gains_imag):
    return (
        (gains_real * real - gains_imag * imag).astype(BF16),
        (gains_real * imag + gains_imag * real).astype(BF16),
    )


def direction_sums(values):
    return jnp.sum(values.reshape(values.shape[0] // P_SIZE, P_SIZE, values.shape[1]), axis=1)


def terms_kernel(
    observed_hbm, catalogue_hbm, order_hbm, gains_hbm, blending_hbm, sums, beams, rows_out,
    observed, catalogue, order, gains, blending, joined, turned, arrived,
):
    copies = [
        pltpu.make_async_copy(source, target, arrived.at[at])
        for at, (source, target) in enumerate(
            (
                (order_hbm, order),
                (catalogue_hbm, catalogue),
                (gains_hbm, gains),
                (observed_hbm, observed),
                (blending_hbm, blending),
            )
        )
    ]
    for copy in copies:
        copy.start()
    copies[0].wait()
    copies[1].wait()
    source = lax.broadcasted_iota(jnp.int32, (N, N), 0)
    pick = jnp.where(source == order[...], 1.0, 0.0).astype(BF16)
    for part in range(2):
        beams[part] = dot(pick, catalogue[part], TN_DIMS).astype(BF16)
    copies[2].wait()
    for half in range(2):
        rows = pl.ds(half * HALF, HALF)
        ks = pl.ds(half * (K // 2), K // 2)
        seeded_real, seeded_imag = rotated_pair(
            beams[0, rows, :].astype(F32),
            beams[1, rows, :].astype(F32),
            expand(gains[0, ks, :]),
            expand(gains[1, ks, :]),
        )
        base = half * 2 * HALF
        joined[pl.ds(base, HALF), :] = seeded_real
        joined[pl.ds(base + HALF, HALF), :] = seeded_imag
        turned[pl.ds(base, HALF), :] = seeded_imag
        turned[pl.ds(base + HALF, HALF), :] = -seeded_real
    row_dir = lax.broadcasted_iota(jnp.int32, (HALF, HALF), 0) // P_SIZE
    col_dir = lax.broadcasted_iota(jnp.int32, (HALF, HALF), 1) // P_SIZE
    same = row_dir == col_dir
    weights = []
    for half in range(2):
        rows = pl.ds(half * HALF, HALF)
        block = joined[pl.ds(half * 2 * HALF, 2 * HALF), :]
        grid = dot(block, block, NT_DIMS)
        gram_real = jnp.where(same, grid[:HALF, :HALF] + grid[HALF:, HALF:], 0.0)
        gram_imag = jnp.where(same, grid[:HALF, HALF:] - grid[HALF:, :HALF], 0.0)
        gram = jnp.concatenate(
            [
                jnp.concatenate([gram_real, gram_imag], axis=1),
                jnp.concatenate([gram_imag, -gram_real], axis=1),
            ],
            axis=0,
        )
        high = gram.astype(BF16)
        low = (gram - high.astype(F32)).astype(BF16)
        both = jnp.concatenate([beams[0, rows, :], beams[1, rows, :]], axis=0)
        inner = dot(high, both, NN_DIMS) + dot(low, both, NN_DIMS)
        real = beams[0, rows, :].astype(F32)
        imag = beams[1, rows, :].astype(F32)
        weights.append(direction_sums(real * inner[:HALF] - imag * inner[HALF:]))
    weight = jnp.concatenate(weights, axis=0)
    everything = joined[...]
    copies[3].wait()
    copies[4].wait()
    rows_out[...] = blending[pl.ds((lax.axis_index("freq") // 2) * 2, 2), :]
    for chunk in range(2):
        cols = pl.ds(chunk * 256, 256)
        model_real = dot(joined[:, cols], everything, TN_DIMS)
        misfit_real = (observed[0, cols, :].astype(F32) - model_real).astype(BF16)
        model_imag = dot(turned[:, cols], everything, TN_DIMS)
        misfit_minus = (model_imag - observed[1, cols, :].astype(F32)).astype(BF16)
        product = dot(everything, misfit_real, NT_DIMS) + dot(turned[...], misfit_minus, NT_DIMS)
        pulls_real, pulls_imag = [], []
        for half in range(2):
            rows = pl.ds(half * HALF, HALF)
            base = half * 2 * HALF
            real = beams[0, rows, cols].astype(F32)
            imag = beams[1, rows, cols].astype(F32)
            product_real = product[base : base + HALF]
            product_imag = product[base + HALF : base + 2 * HALF]
            pulls_real.append(direction_sums(real * product_real + imag * product_imag))
            pulls_imag.append(direction_sums(real * product_imag - imag * product_real))
        weight_here = weight[:, chunk * 256 : chunk * 256 + 256]
        pull_real = jnp.concatenate(pulls_real, axis=0) + 2.0 * gains[0, :, cols] * weight_here
        pull_imag = jnp.concatenate(pulls_imag, axis=0) + 2.0 * gains[1, :, cols] * weight_here
        for group in range(4):
            for side in range(2):
                piece = group * 4 + chunk * 2 + side
                for part, value in enumerate((pull_real, pull_imag, weight_here)):
                    sums[piece, pl.ds(part * 8, 8), :] = value[
                        group * 8 : group * 8 + 8, side * LANES : (side + 1) * LANES
                    ]


def terms(*operands):
    bands = operands[4].shape[0]
    return pl.pallas_call(
        terms_kernel,
        out_shape=(
            jax.ShapeDtypeStruct((16, 24, LANES), F32),
            jax.ShapeDtypeStruct((2, N, S), BF16),
            jax.ShapeDtypeStruct((2, bands), F32),
        ),
        in_specs=[pl.BlockSpec(memory_space=pltpu.HBM)] * 5,
        out_specs=(pl.BlockSpec(memory_space=pltpu.VMEM),) * 3,
        scratch_shapes=[
            pltpu.VMEM((2, S, S), BF16),
            pltpu.VMEM((2, N, S), BF16),
            pltpu.VMEM((1, N), jnp.int32),
            pltpu.VMEM((2, K, S), F32),
            pltpu.VMEM((bands, bands), F32),
            pltpu.VMEM((2 * N, S), BF16),
            pltpu.VMEM((2 * N, S), BF16),
            pltpu.SemaphoreType.DMA((5,)),
        ],
        compiler_params=pltpu.CompilerParams(vmem_limit_bytes=20 * 2**20),
        cost_estimate=pl.CostEstimate(flops=2 * 10**9, bytes_accessed=2 * 10**6, transcendentals=0),
        name="terms",
    )(*[pltpu.with_memory_space_constraint(operand, pltpu.HBM) for operand in operands])


def peel_kernel(
    observed, beams, smooth, residual_hbm, gains_out, residual, joined, turned, sent
):
    for half in range(2):
        rows = pl.ds(half * HALF, HALF)
        base = half * 2 * HALF
        for block in range(4):
            lanes = pl.ds(block * LANES, LANES)
            gains = [
                jnp.concatenate(
                    [expand(smooth[part * 16 + group * 4 + block]) for group in (2 * half, 2 * half + 1)],
                    axis=0,
                )
                for part in range(2)
            ]
            final_real, final_imag = rotated_pair(
                beams[0, rows, lanes].astype(F32), beams[1, rows, lanes].astype(F32), *gains
            )
            joined[pl.ds(base, HALF), lanes] = final_real
            joined[pl.ds(base + HALF, HALF), lanes] = final_imag
            turned[pl.ds(base, HALF), lanes] = final_imag
            turned[pl.ds(base + HALF, HALF), lanes] = -final_real
    everything = joined[...]
    copies = []
    for chunk in range(2):
        cols = pl.ds(chunk * 256, 256)
        for part, left in enumerate((joined, turned)):
            model = dot(left[:, cols], everything, TN_DIMS)
            residual[part, cols, :] = (observed[part, cols, :].astype(F32) - model).astype(BF16)
            copies.append(
                pltpu.make_async_copy(
                    residual.at[part, cols],
                    residual_hbm.at[part, cols],
                    sent.at[2 * chunk + part],
                )
            )
            copies[-1].start()
    slot = lax.axis_index("tm")
    group = slot // 4
    row = (slot % 4) * 2
    for part in range(2):
        for block in range(4):
            gains_out[part, :, pl.ds(block * LANES, LANES)] = smooth[
                part * 16 + group * 4 + block, pl.ds(row, 2), :
            ]
    for copy in copies:
        copy.wait()


def peel(observed, beams, smooth):
    vmem = pl.BlockSpec(memory_space=pltpu.VMEM)
    return pl.pallas_call(
        peel_kernel,
        out_shape=(
            jax.ShapeDtypeStruct((2, S, S), BF16),
            jax.ShapeDtypeStruct((2, 2, S), F32),
        ),
        in_specs=[vmem, vmem, vmem],
        out_specs=(pl.BlockSpec(memory_space=pltpu.HBM), vmem),
        scratch_shapes=[
            pltpu.VMEM((2, S, S), BF16),
            pltpu.VMEM((2 * N, S), BF16),
            pltpu.VMEM((2 * N, S), BF16),
            pltpu.SemaphoreType.DMA((4,)),
        ],
        compiler_params=pltpu.CompilerParams(vmem_limit_bytes=20 * 2**20),
        cost_estimate=pl.CostEstimate(flops=10**9, bytes_accessed=3 * 10**6, transcendentals=0),
        name="peel",
    )(observed, beams, smooth)


def local(observed, source_beams, source_order, initial_gains, blending):
    freqs, times = lax.axis_size("freq"), lax.axis_size("tm")
    observed_block = observed[0, 0]
    sums, beams, rows = terms(
        observed_block,
        source_beams[0, 0],
        source_order.reshape(1, N),
        initial_gains[0],
        blending,
    )
    pieces = lax.all_to_all(sums, "tm", split_axis=0, concat_axis=0, tiled=True)
    totals = jnp.sum(pieces, axis=0).reshape(3, 8, LANES)
    damped = 0.5 * (totals[:2] / totals[2])
    sent = jnp.broadcast_to(damped[None], (freqs // 2, 2, 8, LANES)).reshape(freqs, 8, LANES)
    bands = lax.all_to_all(sent, "freq", split_axis=0, concat_axis=0, tiled=True)
    mixed = jnp.sum(rows[:, :, None, None] * bands[None], axis=1)
    spread = jnp.broadcast_to(mixed[:, None], (2, times, 8, LANES)).reshape(2 * times, 8, LANES)
    groups = [
        [(pair * 2 + core) * times + time for core in range(2) for time in range(times)]
        for pair in range(freqs // 2)
    ]
    smooth = lax.all_to_all(
        spread, ("freq", "tm"), split_axis=0, concat_axis=0, tiled=True, axis_index_groups=groups
    )
    residual, gains_out = peel(observed_block, beams, smooth)
    return (residual[None, None], gains_out[None])


def solution(mesh):
    return jax.shard_map(
        local,
        mesh=mesh,
        in_specs=(
            P("freq", "tm", None, None, None),
            P("freq", "tm", None, None, None),
            P(),
            P("freq", None, None, None),
            P(),
        ),
        out_specs=(P("freq", "tm", None, None, None), P("freq", None, "tm", None)),
        check_vma=False,
    )
```

```python
import jax
import jax.numpy as jnp
from jax import lax
from jax.experimental import pallas as pl
from jax.experimental.pallas import tpu as pltpu
from jax.sharding import PartitionSpec as P

S = 512
K = 32
P_SIZE = 8
N = K * P_SIZE
HALF = 128
GROUP = 16
LANES = 128
NT_DIMS = (((1,), (1,)), ((), ()))
NN_DIMS = (((1,), (0,)), ((), ()))
F32 = jnp.float32
BF16 = jnp.bfloat16


def dot(left, right, dims):
    return lax.dot_general(left, right, dims, preferred_element_type=F32)


def rotated_pair(real, imag, gains_real, gains_imag):
    return gains_real * real - gains_imag * imag, gains_real * imag + gains_imag * real


def repeat_rows(rows):
    return jnp.concatenate([rows] * P_SIZE, axis=0)


def direction_sums(values):
    total = values[:GROUP]
    for at in range(1, P_SIZE):
        total = total + values[at * GROUP : (at + 1) * GROUP]
    return total


def store_pair(wide, half, lanes, real, imag):
    base = half * 2 * HALF
    low, size = lanes
    real, imag = real.astype(BF16), imag.astype(BF16)
    wide[pl.ds(base, HALF), pl.ds(low, size)] = real
    wide[pl.ds(base + HALF, HALF), pl.ds(low, size)] = imag
    wide[pl.ds(base, HALF), pl.ds(S + low, size)] = -imag
    wide[pl.ds(base + HALF, HALF), pl.ds(S + low, size)] = real


def stacked_pair(reals, imags):
    joined, quarter = [], []
    for real, imag in zip(reals, imags):
        real, imag = real.astype(BF16), imag.astype(BF16)
        joined += [real, imag]
        quarter += [-imag, real]
    return jnp.concatenate(joined, axis=0), jnp.concatenate(quarter, axis=0)


def terms_kernel(
    observed_hbm, catalogue_hbm, order_hbm, gains_hbm, blending_hbm, sums, beams, rows_out,
    observed, catalogue, order, gains, blending, exact, wide, turned, misfit, arrived,
):
    copies = [
        pltpu.make_async_copy(source, target, arrived.at[at])
        for at, (source, target) in enumerate(
            (
                (order_hbm, order),
                (catalogue_hbm, catalogue),
                (gains_hbm, gains),
                (observed_hbm, observed),
                (blending_hbm, blending),
            )
        )
    ]
    for copy in copies:
        copy.start()
    copies[0].wait()
    lane = lax.broadcasted_iota(jnp.int32, (2, HALF), 1)
    listed = jnp.take_along_axis(order[...], (lane % GROUP) * P_SIZE + lane // GROUP, axis=1)
    listed = jnp.concatenate([listed[0:1], listed[1:2]], axis=1)
    source = lax.broadcasted_iota(jnp.int32, (N, N), 0)
    pick = jnp.where(source == listed, 1.0, 0.0).astype(BF16).T
    copies[1].wait()
    for part in range(2):
        picked = dot(pick, catalogue[part], NN_DIMS)
        exact[part] = picked
        beams[part] = picked.astype(BF16)
    copies[2].wait()
    copies[3].wait()
    copies[4].wait()
    rows_out[...] = blending[pl.ds((lax.axis_index("freq") // 2) * 2, 2), :]
    for half in range(2):
        rows = pl.ds(half * HALF, HALF)
        ks = pl.ds(half * GROUP, GROUP)
        real, imag = rotated_pair(
            exact[0, rows, :],
            exact[1, rows, :],
            repeat_rows(gains[0, ks, :]),
            repeat_rows(gains[1, ks, :]),
        )
        store_pair(wide, half, (0, S), real, imag)
    turned[...] = wide[:, :S].T
    for part in range(2):
        cols = pl.ds(part * S, S)
        model = dot(turned[...], wide[:, cols], NN_DIMS)
        misfit[:, cols] = (observed[part].astype(F32) - model).astype(BF16)
    everything = dot(wide[...], misfit[...], NT_DIMS)
    row_dir = lax.broadcasted_iota(jnp.int32, (HALF, HALF), 0) % GROUP
    col_dir = lax.broadcasted_iota(jnp.int32, (HALF, HALF), 1) % GROUP
    same = row_dir == col_dir
    weights = []
    for half in range(2):
        rows = pl.ds(half * HALF, HALF)
        block = wide[pl.ds(half * 2 * HALF, 2 * HALF), :S]
        grid = dot(block, block, NT_DIMS)
        gram_real = jnp.where(same, grid[:HALF, :HALF] + grid[HALF:, HALF:], 0.0)
        gram_imag = jnp.where(same, grid[:HALF, HALF:] - grid[HALF:, :HALF], 0.0)
        high_real, high_imag = gram_real.astype(BF16), gram_imag.astype(BF16)
        low_real = (gram_real - high_real.astype(F32)).astype(BF16)
        low_imag = (gram_imag - high_imag.astype(F32)).astype(BF16)
        gram = jnp.concatenate(
            [
                jnp.concatenate([high_real, high_imag, low_real, low_imag], axis=1),
                jnp.concatenate([high_imag, -high_real, low_imag, -low_real], axis=1),
            ],
            axis=0,
        )
        both = jnp.concatenate([beams[0, rows, :], beams[1, rows, :]] * 2, axis=0)
        inner = dot(gram, both, NN_DIMS)
        weights.append(
            direction_sums(exact[0, rows, :] * inner[:HALF] - exact[1, rows, :] * inner[HALF:])
        )
    for half in range(2):
        rows = pl.ds(half * HALF, HALF)
        ks = pl.ds(half * GROUP, GROUP)
        product = everything[half * 2 * HALF : (half + 1) * 2 * HALF]
        real, imag = exact[0, rows, :], exact[1, rows, :]
        weight = weights[half]
        pull_real = direction_sums(real * product[:HALF] + imag * product[HALF:])
        pull_imag = direction_sums(real * product[HALF:] - imag * product[:HALF])
        values = (
            pull_real + 2.0 * gains[0, ks, :] * weight,
            pull_imag + 2.0 * gains[1, ks, :] * weight,
            weight,
        )
        for group in range(2):
            for block in range(4):
                piece = (half * 2 + group) * 4 + block
                for part, value in enumerate(values):
                    sums[piece, pl.ds(part * 8, 8), :] = value[
                        group * 8 : group * 8 + 8, block * LANES : (block + 1) * LANES
                    ]


def terms(*operands):
    bands = operands[4].shape[0]
    return pl.pallas_call(
        terms_kernel,
        out_shape=(
            jax.ShapeDtypeStruct((16, 24, LANES), F32),
            jax.ShapeDtypeStruct((2, N, S), BF16),
            jax.ShapeDtypeStruct((2, bands), F32),
        ),
        in_specs=[pl.BlockSpec(memory_space=pltpu.HBM)] * 5,
        out_specs=(pl.BlockSpec(memory_space=pltpu.VMEM),) * 3,
        scratch_shapes=[
            pltpu.VMEM((2, S, S), BF16),
            pltpu.VMEM((2, N, S), BF16),
            pltpu.VMEM((2, HALF), jnp.int32),
            pltpu.VMEM((2, K, S), F32),
            pltpu.VMEM((bands, bands), F32),
            pltpu.VMEM((2, N, S), F32),
            pltpu.VMEM((2 * N, 2 * S), BF16),
            pltpu.VMEM((S, 2 * N), BF16),
            pltpu.VMEM((S, 2 * S), BF16),
            pltpu.SemaphoreType.DMA((5,)),
        ],
        compiler_params=pltpu.CompilerParams(vmem_limit_bytes=20 * 2**20),
        cost_estimate=pl.CostEstimate(flops=2 * 10**9, bytes_accessed=2 * 10**6, transcendentals=0),
        name="terms",
    )(*[pltpu.with_memory_space_constraint(operand, pltpu.HBM) for operand in operands])


def peel_kernel(observed, beams, smooth, residual_hbm, gains_out, residual, sent):
    pairs = []
    for half in range(2):
        rows = pl.ds(half * HALF, HALF)
        gains = [
            repeat_rows(
                jnp.concatenate(
                    [
                        jnp.concatenate(
                            [smooth[part * 16 + (2 * half + group) * 4 + block] for block in range(4)],
                            axis=1,
                        )
                        for group in range(2)
                    ],
                    axis=0,
                )
            )
            for part in range(2)
        ]
        pairs.append(
            rotated_pair(beams[0, rows, :].astype(F32), beams[1, rows, :].astype(F32), *gains)
        )
    joined, quarter = stacked_pair(*zip(*pairs))
    turned = joined.T
    copies = []
    for part, right in enumerate((joined, quarter)):
        for chunk in range(2):
            cols = pl.ds(chunk * 256, 256)
            model = dot(turned[chunk * 256 : (chunk + 1) * 256], right, NN_DIMS)
            residual[part, cols, :] = (observed[part, cols, :].astype(F32) - model).astype(BF16)
            copies.append(
                pltpu.make_async_copy(
                    residual.at[part, cols],
                    residual_hbm.at[part, cols],
                    sent.at[2 * chunk + part],
                )
            )
            copies[-1].start()
    slot = lax.axis_index("tm")
    group = slot // 4
    row = (slot % 4) * 2
    for part in range(2):
        for block in range(4):
            gains_out[part, :, pl.ds(block * LANES, LANES)] = smooth[
                part * 16 + group * 4 + block, pl.ds(row, 2), :
            ]
    for copy in copies:
        copy.wait()


def peel(observed, beams, smooth):
    vmem = pl.BlockSpec(memory_space=pltpu.VMEM)
    return pl.pallas_call(
        peel_kernel,
        out_shape=(
            jax.ShapeDtypeStruct((2, S, S), BF16),
            jax.ShapeDtypeStruct((2, 2, S), F32),
        ),
        in_specs=[vmem, vmem, vmem],
        out_specs=(pl.BlockSpec(memory_space=pltpu.HBM), vmem),
        scratch_shapes=[
            pltpu.VMEM((2, S, S), BF16),
            pltpu.SemaphoreType.DMA((4,)),
        ],
        compiler_params=pltpu.CompilerParams(vmem_limit_bytes=20 * 2**20),
        cost_estimate=pl.CostEstimate(flops=10**9, bytes_accessed=3 * 10**6, transcendentals=0),
        name="peel",
    )(observed, beams, smooth)


def local(observed, source_beams, source_order, initial_gains, blending):
    freqs, times = lax.axis_size("freq"), lax.axis_size("tm")
    observed_block = observed[0, 0]
    sums, beams, rows = terms(
        observed_block,
        source_beams[0, 0],
        source_order.reshape(2, HALF),
        initial_gains[0],
        blending,
    )
    pieces = lax.all_to_all(sums, "tm", split_axis=0, concat_axis=0, tiled=True)
    totals = jnp.sum(pieces, axis=0).reshape(3, 8, LANES)
    damped = 0.5 * (totals[:2] / totals[2])
    sent = jnp.broadcast_to(damped[None], (freqs // 2, 2, 8, LANES)).reshape(freqs, 8, LANES)
    bands = lax.all_to_all(sent, "freq", split_axis=0, concat_axis=0, tiled=True)
    mixed = jnp.sum(rows[:, :, None, None] * bands[None], axis=1)
    spread = jnp.broadcast_to(mixed[:, None], (2, times, 8, LANES)).reshape(2 * times, 8, LANES)
    groups = [
        [(pair * 2 + core) * times + time for core in range(2) for time in range(times)]
        for pair in range(freqs // 2)
    ]
    smooth = lax.all_to_all(
        spread, ("freq", "tm"), split_axis=0, concat_axis=0, tiled=True, axis_index_groups=groups
    )
    residual, gains_out = peel(observed_block, beams, smooth)
    return (residual[None, None], gains_out[None])


def solution(mesh):
    return jax.shard_map(
        local,
        mesh=mesh,
        in_specs=(
            P("freq", "tm", None, None, None),
            P("freq", "tm", None, None, None),
            P(),
            P("freq", None, None, None),
            P(),
        ),
        out_specs=(P("freq", "tm", None, None, None), P("freq", None, "tm", None)),
        check_vma=False,
    )
```

```python
import jax
import jax.numpy as jnp
from jax import lax
from jax.experimental import pallas as pl
from jax.experimental.pallas import tpu as pltpu
from jax.sharding import PartitionSpec as P

S = 512
K = 32
P_SIZE = 8
N = K * P_SIZE
HALF = 128
GROUP = 16
LANES = 128
TEAM = 4
QUARTER = 4
NT_DIMS = (((1,), (1,)), ((), ()))
NN_DIMS = (((1,), (0,)), ((), ()))
F32 = jnp.float32
BF16 = jnp.bfloat16


def dot(left, right, dims):
    return lax.dot_general(left, right, dims, preferred_element_type=F32)


def rotated_pair(real, imag, gains_real, gains_imag):
    return gains_real * real - gains_imag * imag, gains_real * imag + gains_imag * real


def repeat_rows(rows):
    return jnp.concatenate([rows] * P_SIZE, axis=0)


def direction_sums(values):
    total = values[:GROUP]
    for at in range(1, P_SIZE):
        total = total + values[at * GROUP : (at + 1) * GROUP]
    return total


def store_pair(wide, half, lanes, real, imag):
    base = half * 2 * HALF
    low, size = lanes
    real, imag = real.astype(BF16), imag.astype(BF16)
    wide[pl.ds(base, HALF), pl.ds(low, size)] = real
    wide[pl.ds(base + HALF, HALF), pl.ds(low, size)] = imag
    wide[pl.ds(base, HALF), pl.ds(S + low, size)] = -imag
    wide[pl.ds(base + HALF, HALF), pl.ds(S + low, size)] = real


def stacked_pair(reals, imags):
    joined, quarter = [], []
    for real, imag in zip(reals, imags):
        real, imag = real.astype(BF16), imag.astype(BF16)
        joined += [real, imag]
        quarter += [-imag, real]
    return jnp.concatenate(joined, axis=0), jnp.concatenate(quarter, axis=0)


def terms_kernel(
    observed_hbm, catalogue_hbm, order_hbm, gains_hbm, blending_hbm, sums, beams, rows_out,
    observed, catalogue, order, gains, blending, exact, wide, turned, misfit, arrived,
):
    copies = [
        pltpu.make_async_copy(source, target, arrived.at[at])
        for at, (source, target) in enumerate(
            (
                (order_hbm, order),
                (catalogue_hbm, catalogue),
                (gains_hbm, gains),
                (observed_hbm, observed),
                (blending_hbm, blending),
            )
        )
    ]
    for copy in copies:
        copy.start()
    copies[0].wait()
    lane = lax.broadcasted_iota(jnp.int32, (2, HALF), 1)
    listed = jnp.take_along_axis(order[...], (lane % GROUP) * P_SIZE + lane // GROUP, axis=1)
    listed = jnp.concatenate([listed[0:1], listed[1:2]], axis=1)
    source = lax.broadcasted_iota(jnp.int32, (N, N), 0)
    pick = jnp.where(source == listed, 1.0, 0.0).astype(BF16).T
    copies[1].wait()
    for part in range(2):
        picked = dot(pick, catalogue[part], NN_DIMS)
        exact[part] = picked
        beams[part] = picked.astype(BF16)
    copies[2].wait()
    copies[3].wait()
    copies[4].wait()
    rows_out[...] = blending[pl.ds((lax.axis_index("freq") // TEAM) * TEAM, TEAM), :]
    for half in range(2):
        rows = pl.ds(half * HALF, HALF)
        ks = pl.ds(half * GROUP, GROUP)
        real, imag = rotated_pair(
            exact[0, rows, :],
            exact[1, rows, :],
            repeat_rows(gains[0, ks, :]),
            repeat_rows(gains[1, ks, :]),
        )
        store_pair(wide, half, (0, S), real, imag)
    turned[...] = wide[:, :S].T
    for part in range(2):
        cols = pl.ds(part * S, S)
        model = dot(turned[...], wide[:, cols], NN_DIMS)
        misfit[:, cols] = (observed[part].astype(F32) - model).astype(BF16)
    everything = dot(wide[...], misfit[...], NT_DIMS)
    row_dir = lax.broadcasted_iota(jnp.int32, (HALF, HALF), 0) % GROUP
    col_dir = lax.broadcasted_iota(jnp.int32, (HALF, HALF), 1) % GROUP
    same = row_dir == col_dir
    weights = []
    for half in range(2):
        rows = pl.ds(half * HALF, HALF)
        block = wide[pl.ds(half * 2 * HALF, 2 * HALF), :S]
        grid = dot(block, block, NT_DIMS)
        gram_real = jnp.where(same, grid[:HALF, :HALF] + grid[HALF:, HALF:], 0.0)
        gram_imag = jnp.where(same, grid[:HALF, HALF:] - grid[HALF:, :HALF], 0.0)
        high_real, high_imag = gram_real.astype(BF16), gram_imag.astype(BF16)
        low_real = (gram_real - high_real.astype(F32)).astype(BF16)
        low_imag = (gram_imag - high_imag.astype(F32)).astype(BF16)
        gram = jnp.concatenate(
            [
                jnp.concatenate([high_real, high_imag, low_real, low_imag], axis=1),
                jnp.concatenate([high_imag, -high_real, low_imag, -low_real], axis=1),
            ],
            axis=0,
        )
        both = jnp.concatenate([beams[0, rows, :], beams[1, rows, :]] * 2, axis=0)
        inner = dot(gram, both, NN_DIMS)
        weights.append(
            direction_sums(exact[0, rows, :] * inner[:HALF] - exact[1, rows, :] * inner[HALF:])
        )
    for half in range(2):
        rows = pl.ds(half * HALF, HALF)
        ks = pl.ds(half * GROUP, GROUP)
        product = everything[half * 2 * HALF : (half + 1) * 2 * HALF]
        real, imag = exact[0, rows, :], exact[1, rows, :]
        weight = weights[half]
        pull_real = direction_sums(real * product[:HALF] + imag * product[HALF:])
        pull_imag = direction_sums(real * product[HALF:] - imag * product[:HALF])
        values = (
            pull_real + 2.0 * gains[0, ks, :] * weight,
            pull_imag + 2.0 * gains[1, ks, :] * weight,
            weight,
        )
        for group in range(2):
            for block in range(4):
                piece = (half * 2 + group) * 4 + block
                for part, value in enumerate(values):
                    sums[piece, pl.ds(part * 8, 8), :] = value[
                        group * 8 : group * 8 + 8, block * LANES : (block + 1) * LANES
                    ]


def terms(*operands):
    bands = operands[4].shape[0]
    return pl.pallas_call(
        terms_kernel,
        out_shape=(
            jax.ShapeDtypeStruct((16, 24, LANES), F32),
            jax.ShapeDtypeStruct((2, N, S), BF16),
            jax.ShapeDtypeStruct((TEAM, bands), F32),
        ),
        in_specs=[pl.BlockSpec(memory_space=pltpu.HBM)] * 5,
        out_specs=(pl.BlockSpec(memory_space=pltpu.VMEM),) * 3,
        scratch_shapes=[
            pltpu.VMEM((2, S, S), BF16),
            pltpu.VMEM((2, N, S), BF16),
            pltpu.VMEM((2, HALF), jnp.int32),
            pltpu.VMEM((2, K, S), F32),
            pltpu.VMEM((bands, bands), F32),
            pltpu.VMEM((2, N, S), F32),
            pltpu.VMEM((2 * N, 2 * S), BF16),
            pltpu.VMEM((S, 2 * N), BF16),
            pltpu.VMEM((S, 2 * S), BF16),
            pltpu.SemaphoreType.DMA((5,)),
        ],
        compiler_params=pltpu.CompilerParams(vmem_limit_bytes=20 * 2**20),
        cost_estimate=pl.CostEstimate(flops=2 * 10**9, bytes_accessed=2 * 10**6, transcendentals=0),
        name="terms",
    )(*[pltpu.with_memory_space_constraint(operand, pltpu.HBM) for operand in operands])


def peel_kernel(observed, beams, smooth, residual_hbm, gains_out, residual, sent):
    pairs = []
    for half in range(2):
        rows = pl.ds(half * HALF, HALF)
        gains = [
            repeat_rows(
                jnp.concatenate(
                    [
                        jnp.concatenate(
                            [
                                smooth[(part * 2 + low) * 16 + (2 * half + group) * 4 + block]
                                for block in range(4)
                            ],
                            axis=1,
                        )
                        for group in range(2)
                        for low in range(2)
                    ],
                    axis=0,
                )
            )
            for part in range(2)
        ]
        pairs.append(
            rotated_pair(beams[0, rows, :].astype(F32), beams[1, rows, :].astype(F32), *gains)
        )
    joined, quarter = stacked_pair(*zip(*pairs))
    turned = joined.T
    copies = []
    for part, right in enumerate((joined, quarter)):
        for chunk in range(2):
            cols = pl.ds(chunk * 256, 256)
            model = dot(turned[chunk * 256 : (chunk + 1) * 256], right, NN_DIMS)
            residual[part, cols, :] = (observed[part, cols, :].astype(F32) - model).astype(BF16)
            copies.append(
                pltpu.make_async_copy(
                    residual.at[part, cols],
                    residual_hbm.at[part, cols],
                    sent.at[2 * chunk + part],
                )
            )
            copies[-1].start()
    slot = lax.axis_index("tm")
    group = slot // 4
    low = (slot % 4) // 2
    row = (slot % 2) * 2
    for part in range(2):
        for block in range(4):
            gains_out[part, :, pl.ds(block * LANES, LANES)] = smooth[
                (part * 2 + low) * 16 + group * 4 + block, pl.ds(row, 2), :
            ]
    for copy in copies:
        copy.wait()


def peel(observed, beams, smooth):
    vmem = pl.BlockSpec(memory_space=pltpu.VMEM)
    return pl.pallas_call(
        peel_kernel,
        out_shape=(
            jax.ShapeDtypeStruct((2, S, S), BF16),
            jax.ShapeDtypeStruct((2, 2, S), F32),
        ),
        in_specs=[vmem, vmem, vmem],
        out_specs=(pl.BlockSpec(memory_space=pltpu.HBM), vmem),
        scratch_shapes=[
            pltpu.VMEM((2, S, S), BF16),
            pltpu.SemaphoreType.DMA((4,)),
        ],
        compiler_params=pltpu.CompilerParams(vmem_limit_bytes=20 * 2**20),
        cost_estimate=pl.CostEstimate(flops=10**9, bytes_accessed=3 * 10**6, transcendentals=0),
        name="peel",
    )(observed, beams, smooth)


def local(observed, source_beams, source_order, initial_gains, blending):
    freqs, times = lax.axis_size("freq"), lax.axis_size("tm")
    observed_block = observed[0, 0]
    sums, beams, rows = terms(
        observed_block,
        source_beams[0, 0],
        source_order.reshape(2, HALF),
        initial_gains[0],
        blending,
    )
    pieces = lax.all_to_all(sums, "tm", split_axis=0, concat_axis=0, tiled=True)
    totals = jnp.sum(pieces, axis=0).reshape(3, 8, LANES)
    damped = 0.5 * (totals[:2] / totals[2])
    quarters = damped.reshape(TEAM, QUARTER, LANES)
    sent = jnp.broadcast_to(quarters[None], (freqs // TEAM, TEAM, QUARTER, LANES))
    bands = lax.all_to_all(
        sent.reshape(freqs, QUARTER, LANES), "freq", split_axis=0, concat_axis=0, tiled=True
    )
    mixed = jnp.sum(rows[:, :, None, None] * bands[None], axis=1)
    spread = jnp.broadcast_to(mixed[:, None], (TEAM, times, QUARTER, LANES))
    groups = [
        [(team * TEAM + member) * times + time for member in range(TEAM) for time in range(times)]
        for team in range(freqs // TEAM)
    ]
    smooth = lax.all_to_all(
        spread.reshape(TEAM * times, QUARTER, LANES),
        ("freq", "tm"),
        split_axis=0,
        concat_axis=0,
        tiled=True,
        axis_index_groups=groups,
    )
    residual, gains_out = peel(observed_block, beams, smooth)
    return (residual[None, None], gains_out[None])


def solution(mesh):
    return jax.shard_map(
        local,
        mesh=mesh,
        in_specs=(
            P("freq", "tm", None, None, None),
            P("freq", "tm", None, None, None),
            P(),
            P("freq", None, None, None),
            P(),
        ),
        out_specs=(P("freq", "tm", None, None, None), P("freq", None, "tm", None)),
        check_vma=False,
    )
```

```python
import jax
import jax.numpy as jnp
from jax import lax
from jax.experimental import pallas as pl
from jax.experimental.pallas import tpu as pltpu
from jax.sharding import PartitionSpec as P

S = 512
K = 32
P_SIZE = 8
N = K * P_SIZE
HALF = 128
GROUP = 16
LANES = 128
TEAM = 4
QUARTER = 4
NT_DIMS = (((1,), (1,)), ((), ()))
NN_DIMS = (((1,), (0,)), ((), ()))
F32 = jnp.float32
BF16 = jnp.bfloat16


def dot(left, right, dims):
    return lax.dot_general(left, right, dims, preferred_element_type=F32)


def rotated_pair(real, imag, gains_real, gains_imag):
    return gains_real * real - gains_imag * imag, gains_real * imag + gains_imag * real


def repeat_rows(rows):
    return jnp.concatenate([rows] * P_SIZE, axis=0)


def direction_sums(values):
    total = values[:GROUP]
    for at in range(1, P_SIZE):
        total = total + values[at * GROUP : (at + 1) * GROUP]
    return total


def store_pair(wide, half, lanes, real, imag):
    base = half * 2 * HALF
    low, size = lanes
    real, imag = real.astype(BF16), imag.astype(BF16)
    wide[pl.ds(base, HALF), pl.ds(low, size)] = real
    wide[pl.ds(base + HALF, HALF), pl.ds(low, size)] = imag
    wide[pl.ds(base, HALF), pl.ds(S + low, size)] = -imag
    wide[pl.ds(base + HALF, HALF), pl.ds(S + low, size)] = real


def stacked_pair(reals, imags):
    joined, quarter = [], []
    for real, imag in zip(reals, imags):
        real, imag = real.astype(BF16), imag.astype(BF16)
        joined += [real, imag]
        quarter += [-imag, real]
    return jnp.concatenate(joined, axis=0), jnp.concatenate(quarter, axis=0)


def terms_kernel(
    observed_hbm, catalogue_hbm, order_hbm, gains_hbm, blending_hbm, sums, beams, rows_out,
    observed, catalogue, order, gains, blending, exact, wide, turned, misfit, arrived,
):
    copies = [
        pltpu.make_async_copy(source, target, arrived.at[at])
        for at, (source, target) in enumerate(
            (
                (order_hbm, order),
                (catalogue_hbm, catalogue),
                (gains_hbm, gains),
                (observed_hbm, observed),
                (blending_hbm, blending),
            )
        )
    ]
    for copy in copies:
        copy.start()
    copies[0].wait()
    lane = lax.broadcasted_iota(jnp.int32, (2, HALF), 1)
    listed = jnp.take_along_axis(order[...], (lane % GROUP) * P_SIZE + lane // GROUP, axis=1)
    listed = jnp.concatenate([listed[0:1], listed[1:2]], axis=1)
    source = lax.broadcasted_iota(jnp.int32, (N, N), 0)
    pick = jnp.where(source == listed, 1.0, 0.0).astype(BF16).T
    copies[1].wait()
    for part in range(2):
        picked = dot(pick, catalogue[part], NN_DIMS)
        exact[part] = picked
        beams[part] = picked.astype(BF16)
    copies[2].wait()
    copies[3].wait()
    copies[4].wait()
    rows_out[...] = blending[pl.ds((lax.axis_index("freq") // TEAM) * TEAM, TEAM), :]
    for half in range(2):
        rows = pl.ds(half * HALF, HALF)
        ks = pl.ds(half * GROUP, GROUP)
        real, imag = rotated_pair(
            exact[0, rows, :],
            exact[1, rows, :],
            repeat_rows(gains[0, ks, :]),
            repeat_rows(gains[1, ks, :]),
        )
        store_pair(wide, half, (0, S), real, imag)
    turned[...] = wide[:, :S].T
    for part in range(2):
        cols = pl.ds(part * S, S)
        model = dot(turned[...], wide[:, cols], NN_DIMS)
        misfit[:, cols] = (observed[part].astype(F32) - model).astype(BF16)
    everything = dot(wide[...], misfit[...], NT_DIMS)
    row_dir = lax.broadcasted_iota(jnp.int32, (HALF, HALF), 0) % GROUP
    col_dir = lax.broadcasted_iota(jnp.int32, (HALF, HALF), 1) % GROUP
    same = row_dir == col_dir
    weights = []
    for half in range(2):
        rows = pl.ds(half * HALF, HALF)
        block = wide[pl.ds(half * 2 * HALF, 2 * HALF), :S]
        grid = dot(block, block, NT_DIMS)
        gram_real = jnp.where(same, grid[:HALF, :HALF] + grid[HALF:, HALF:], 0.0)
        gram_imag = jnp.where(same, grid[:HALF, HALF:] - grid[HALF:, :HALF], 0.0)
        high_real, high_imag = gram_real.astype(BF16), gram_imag.astype(BF16)
        low_real = (gram_real - high_real.astype(F32)).astype(BF16)
        low_imag = (gram_imag - high_imag.astype(F32)).astype(BF16)
        gram = jnp.concatenate(
            [
                jnp.concatenate([high_real, high_imag, low_real, low_imag], axis=1),
                jnp.concatenate([high_imag, -high_real, low_imag, -low_real], axis=1),
            ],
            axis=0,
        )
        both = jnp.concatenate([beams[0, rows, :], beams[1, rows, :]] * 2, axis=0)
        inner = dot(gram, both, NN_DIMS)
        weights.append(
            direction_sums(exact[0, rows, :] * inner[:HALF] - exact[1, rows, :] * inner[HALF:])
        )
    for half in range(2):
        rows = pl.ds(half * HALF, HALF)
        ks = pl.ds(half * GROUP, GROUP)
        product = everything[half * 2 * HALF : (half + 1) * 2 * HALF]
        real, imag = exact[0, rows, :], exact[1, rows, :]
        weight = weights[half]
        pull_real = direction_sums(real * product[:HALF] + imag * product[HALF:])
        pull_imag = direction_sums(real * product[HALF:] - imag * product[:HALF])
        values = (
            pull_real + 2.0 * gains[0, ks, :] * weight,
            pull_imag + 2.0 * gains[1, ks, :] * weight,
            weight,
        )
        for group in range(2):
            for block in range(4):
                piece = (half * 2 + group) * 4 + block
                for part, value in enumerate(values):
                    sums[piece, pl.ds(part * 8, 8), :] = value[
                        group * 8 : group * 8 + 8, block * LANES : (block + 1) * LANES
                    ]


def terms(*operands):
    bands = operands[4].shape[0]
    return pl.pallas_call(
        terms_kernel,
        out_shape=(
            jax.ShapeDtypeStruct((16, 24, LANES), F32),
            jax.ShapeDtypeStruct((2, N, S), BF16),
            jax.ShapeDtypeStruct((TEAM, bands), F32),
        ),
        in_specs=[pl.BlockSpec(memory_space=pltpu.HBM)] * 5,
        out_specs=(pl.BlockSpec(memory_space=pltpu.VMEM),) * 3,
        scratch_shapes=[
            pltpu.VMEM((2, S, S), BF16),
            pltpu.VMEM((2, N, S), BF16),
            pltpu.VMEM((2, HALF), jnp.int32),
            pltpu.VMEM((2, K, S), F32),
            pltpu.VMEM((bands, bands), F32),
            pltpu.VMEM((2, N, S), F32),
            pltpu.VMEM((2 * N, 2 * S), BF16),
            pltpu.VMEM((S, 2 * N), BF16),
            pltpu.VMEM((S, 2 * S), BF16),
            pltpu.SemaphoreType.DMA((5,)),
        ],
        compiler_params=pltpu.CompilerParams(vmem_limit_bytes=20 * 2**20),
        cost_estimate=pl.CostEstimate(flops=2 * 10**9, bytes_accessed=2 * 10**6, transcendentals=0),
        name="terms",
    )(*[pltpu.with_memory_space_constraint(operand, pltpu.HBM) for operand in operands])


def peel_kernel(observed, beams, smooth, residual_hbm, gains_hbm, residual, gains_out, sent):
    slot = lax.axis_index("tm")
    group = slot // 4
    low = (slot % 4) // 2
    row = (slot % 2) * 2
    for part in range(2):
        for block in range(4):
            gains_out[part, :, pl.ds(block * LANES, LANES)] = smooth[
                (part * 2 + low) * 16 + group * 4 + block, pl.ds(row, 2), :
            ]
    copies = [pltpu.make_async_copy(gains_out, gains_hbm, sent.at[4])]
    copies[0].start()
    pairs = []
    for half in range(2):
        rows = pl.ds(half * HALF, HALF)
        gains = [
            repeat_rows(
                jnp.concatenate(
                    [
                        jnp.concatenate(
                            [
                                smooth[(part * 2 + low) * 16 + (2 * half + group) * 4 + block]
                                for block in range(4)
                            ],
                            axis=1,
                        )
                        for group in range(2)
                        for low in range(2)
                    ],
                    axis=0,
                )
            )
            for part in range(2)
        ]
        pairs.append(
            rotated_pair(beams[0, rows, :].astype(F32), beams[1, rows, :].astype(F32), *gains)
        )
    joined, quarter = stacked_pair(*zip(*pairs))
    turned = joined.T
    for part, right in enumerate((joined, quarter)):
        for chunk in range(2):
            cols = pl.ds(chunk * 256, 256)
            model = dot(turned[chunk * 256 : (chunk + 1) * 256], right, NN_DIMS)
            residual[part, cols, :] = (observed[part, cols, :].astype(F32) - model).astype(BF16)
            copies.append(
                pltpu.make_async_copy(
                    residual.at[part, cols],
                    residual_hbm.at[part, cols],
                    sent.at[2 * chunk + part],
                )
            )
            copies[-1].start()
    for copy in copies:
        copy.wait()


def peel(observed, beams, smooth):
    vmem = pl.BlockSpec(memory_space=pltpu.VMEM)
    return pl.pallas_call(
        peel_kernel,
        out_shape=(
            jax.ShapeDtypeStruct((2, S, S), BF16),
            jax.ShapeDtypeStruct((2, 2, S), F32),
        ),
        in_specs=[vmem, vmem, vmem],
        out_specs=(pl.BlockSpec(memory_space=pltpu.HBM),) * 2,
        scratch_shapes=[
            pltpu.VMEM((2, S, S), BF16),
            pltpu.VMEM((2, 2, S), F32),
            pltpu.SemaphoreType.DMA((5,)),
        ],
        compiler_params=pltpu.CompilerParams(vmem_limit_bytes=20 * 2**20),
        cost_estimate=pl.CostEstimate(flops=10**9, bytes_accessed=3 * 10**6, transcendentals=0),
        name="peel",
    )(observed, beams, smooth)


def local(observed, source_beams, source_order, initial_gains, blending):
    freqs, times = lax.axis_size("freq"), lax.axis_size("tm")
    observed_block = observed[0, 0]
    sums, beams, rows = terms(
        observed_block,
        source_beams[0, 0],
        source_order.reshape(2, HALF),
        initial_gains[0],
        blending,
    )
    pieces = lax.all_to_all(sums, "tm", split_axis=0, concat_axis=0, tiled=True)
    totals = jnp.sum(pieces, axis=0).reshape(3, 8, LANES)
    damped = 0.5 * (totals[:2] / totals[2])
    quarters = damped.reshape(TEAM, QUARTER, LANES)
    sent = jnp.broadcast_to(quarters[None], (freqs // TEAM, TEAM, QUARTER, LANES))
    bands = lax.all_to_all(
        sent.reshape(freqs, QUARTER, LANES), "freq", split_axis=0, concat_axis=0, tiled=True
    )
    mixed = jnp.sum(rows[:, :, None, None] * bands[None], axis=1)
    spread = jnp.broadcast_to(mixed[:, None], (TEAM, times, QUARTER, LANES))
    groups = [
        [(team * TEAM + member) * times + time for member in range(TEAM) for time in range(times)]
        for team in range(freqs // TEAM)
    ]
    smooth = lax.all_to_all(
        spread.reshape(TEAM * times, QUARTER, LANES),
        ("freq", "tm"),
        split_axis=0,
        concat_axis=0,
        tiled=True,
        axis_index_groups=groups,
    )
    residual, gains_out = peel(observed_block, beams, smooth)
    return (residual[None, None], gains_out[None])


def solution(mesh):
    return jax.shard_map(
        local,
        mesh=mesh,
        in_specs=(
            P("freq", "tm", None, None, None),
            P("freq", "tm", None, None, None),
            P(),
            P("freq", None, None, None),
            P(),
        ),
        out_specs=(P("freq", "tm", None, None, None), P("freq", None, "tm", None)),
        check_vma=False,
    )
```

```python
import jax
import jax.numpy as jnp
from jax import lax
from jax.experimental import pallas as pl
from jax.experimental.pallas import tpu as pltpu
from jax.sharding import PartitionSpec as P

S = 512
K = 32
P_SIZE = 8
N = K * P_SIZE
HALF = 128
GROUP = 16
LANES = 128
TEAM = 4
NT_DIMS = (((1,), (1,)), ((), ()))
NN_DIMS = (((1,), (0,)), ((), ()))
F32 = jnp.float32
BF16 = jnp.bfloat16


def dot(left, right, dims):
    return lax.dot_general(left, right, dims, preferred_element_type=F32)


def rotated_pair(real, imag, gains_real, gains_imag):
    return gains_real * real - gains_imag * imag, gains_real * imag + gains_imag * real


def repeat_rows(rows):
    return jnp.concatenate([rows] * P_SIZE, axis=0)


def direction_sums(values):
    total = values[:GROUP]
    for at in range(1, P_SIZE):
        total = total + values[at * GROUP : (at + 1) * GROUP]
    return total


def store_pair(wide, half, lanes, real, imag):
    base = half * 2 * HALF
    low, size = lanes
    real, imag = real.astype(BF16), imag.astype(BF16)
    wide[pl.ds(base, HALF), pl.ds(low, size)] = real
    wide[pl.ds(base + HALF, HALF), pl.ds(low, size)] = imag
    wide[pl.ds(base, HALF), pl.ds(S + low, size)] = -imag
    wide[pl.ds(base + HALF, HALF), pl.ds(S + low, size)] = real


def stacked_pair(reals, imags):
    joined, quarter = [], []
    for real, imag in zip(reals, imags):
        real, imag = real.astype(BF16), imag.astype(BF16)
        joined += [real, imag]
        quarter += [-imag, real]
    return jnp.concatenate(joined, axis=0), jnp.concatenate(quarter, axis=0)


def terms_kernel(
    observed_hbm, catalogue_hbm, order_hbm, gains_hbm, blending_hbm, sums, beams, rows_out,
    observed, catalogue, order, gains, blending, exact, wide, turned, misfit, arrived,
):
    copies = [
        pltpu.make_async_copy(source, target, arrived.at[at])
        for at, (source, target) in enumerate(
            (
                (order_hbm, order),
                (catalogue_hbm, catalogue),
                (gains_hbm, gains),
                (observed_hbm, observed),
                (blending_hbm, blending),
            )
        )
    ]
    for copy in copies:
        copy.start()
    copies[0].wait()
    lane = lax.broadcasted_iota(jnp.int32, (2, HALF), 1)
    listed = jnp.take_along_axis(order[...], (lane % GROUP) * P_SIZE + lane // GROUP, axis=1)
    listed = jnp.concatenate([listed[0:1], listed[1:2]], axis=1)
    source = lax.broadcasted_iota(jnp.int32, (N, N), 0)
    pick = jnp.where(source == listed, 1.0, 0.0).astype(BF16).T
    copies[1].wait()
    for part in range(2):
        picked = dot(pick, catalogue[part], NN_DIMS)
        exact[part] = picked
        beams[part] = picked.astype(BF16)
    copies[2].wait()
    copies[3].wait()
    copies[4].wait()
    freq = lax.axis_index("freq")
    first = freq - 2 * ((freq // 2) % 2)
    rows_out[...] = jnp.concatenate([blending[pl.ds(first, 1), :], blending[pl.ds(first + 2, 1), :]], axis=0)
    for half in range(2):
        rows = pl.ds(half * HALF, HALF)
        ks = pl.ds(half * GROUP, GROUP)
        real, imag = rotated_pair(
            exact[0, rows, :],
            exact[1, rows, :],
            repeat_rows(gains[0, ks, :]),
            repeat_rows(gains[1, ks, :]),
        )
        store_pair(wide, half, (0, S), real, imag)
    turned[...] = wide[:, :S].T
    for part in range(2):
        cols = pl.ds(part * S, S)
        model = dot(turned[...], wide[:, cols], NN_DIMS)
        misfit[:, cols] = (observed[part].astype(F32) - model).astype(BF16)
    everything = dot(wide[...], misfit[...], NT_DIMS)
    row_dir = lax.broadcasted_iota(jnp.int32, (HALF, HALF), 0) % GROUP
    col_dir = lax.broadcasted_iota(jnp.int32, (HALF, HALF), 1) % GROUP
    same = row_dir == col_dir
    weights = []
    for half in range(2):
        rows = pl.ds(half * HALF, HALF)
        block = wide[pl.ds(half * 2 * HALF, 2 * HALF), :S]
        grid = dot(block, block, NT_DIMS)
        gram_real = jnp.where(same, grid[:HALF, :HALF] + grid[HALF:, HALF:], 0.0)
        gram_imag = jnp.where(same, grid[:HALF, HALF:] - grid[HALF:, :HALF], 0.0)
        high_real, high_imag = gram_real.astype(BF16), gram_imag.astype(BF16)
        low_real = (gram_real - high_real.astype(F32)).astype(BF16)
        low_imag = (gram_imag - high_imag.astype(F32)).astype(BF16)
        gram = jnp.concatenate(
            [
                jnp.concatenate([high_real, high_imag, low_real, low_imag], axis=1),
                jnp.concatenate([high_imag, -high_real, low_imag, -low_real], axis=1),
            ],
            axis=0,
        )
        both = jnp.concatenate([beams[0, rows, :], beams[1, rows, :]] * 2, axis=0)
        inner = dot(gram, both, NN_DIMS)
        weights.append(
            direction_sums(exact[0, rows, :] * inner[:HALF] - exact[1, rows, :] * inner[HALF:])
        )
    for half in range(2):
        rows = pl.ds(half * HALF, HALF)
        ks = pl.ds(half * GROUP, GROUP)
        product = everything[half * 2 * HALF : (half + 1) * 2 * HALF]
        real, imag = exact[0, rows, :], exact[1, rows, :]
        weight = weights[half]
        pull_real = direction_sums(real * product[:HALF] + imag * product[HALF:])
        pull_imag = direction_sums(real * product[HALF:] - imag * product[:HALF])
        values = (
            pull_real + 2.0 * gains[0, ks, :] * weight,
            pull_imag + 2.0 * gains[1, ks, :] * weight,
            weight,
        )
        for group in range(2):
            for block in range(4):
                piece = (half * 2 + group) * 4 + block
                for part, value in enumerate(values):
                    sums[piece, pl.ds(part * 8, 8), :] = value[
                        group * 8 : group * 8 + 8, block * LANES : (block + 1) * LANES
                    ]


def terms(*operands):
    bands = operands[4].shape[0]
    return pl.pallas_call(
        terms_kernel,
        out_shape=(
            jax.ShapeDtypeStruct((16, 24, LANES), F32),
            jax.ShapeDtypeStruct((2, N, S), BF16),
            jax.ShapeDtypeStruct((2, bands), F32),
        ),
        in_specs=[pl.BlockSpec(memory_space=pltpu.HBM)] * 5,
        out_specs=(pl.BlockSpec(memory_space=pltpu.VMEM),) * 3,
        scratch_shapes=[
            pltpu.VMEM((2, S, S), BF16),
            pltpu.VMEM((2, N, S), BF16),
            pltpu.VMEM((2, HALF), jnp.int32),
            pltpu.VMEM((2, K, S), F32),
            pltpu.VMEM((bands, bands), F32),
            pltpu.VMEM((2, N, S), F32),
            pltpu.VMEM((2 * N, 2 * S), BF16),
            pltpu.VMEM((S, 2 * N), BF16),
            pltpu.VMEM((S, 2 * S), BF16),
            pltpu.SemaphoreType.DMA((5,)),
        ],
        compiler_params=pltpu.CompilerParams(vmem_limit_bytes=20 * 2**20),
        cost_estimate=pl.CostEstimate(flops=2 * 10**9, bytes_accessed=2 * 10**6, transcendentals=0),
        name="terms",
    )(*[pltpu.with_memory_space_constraint(operand, pltpu.HBM) for operand in operands])


def peel_kernel(observed, beams, smooth, residual_hbm, gains_hbm, residual, gains_out, sent):
    slot = lax.axis_index("tm")
    group = slot // 4
    row = (slot % 4) * 2
    for part in range(2):
        for block in range(4):
            gains_out[part, :, pl.ds(block * LANES, LANES)] = smooth[
                part * 16 + group * 4 + block, pl.ds(row, 2), :
            ]
    copies = [pltpu.make_async_copy(gains_out, gains_hbm, sent.at[4])]
    copies[0].start()
    pairs = []
    for half in range(2):
        rows = pl.ds(half * HALF, HALF)
        gains = [
            repeat_rows(
                jnp.concatenate(
                    [
                        jnp.concatenate(
                            [smooth[part * 16 + (2 * half + group) * 4 + block] for block in range(4)],
                            axis=1,
                        )
                        for group in range(2)
                    ],
                    axis=0,
                )
            )
            for part in range(2)
        ]
        pairs.append(
            rotated_pair(beams[0, rows, :].astype(F32), beams[1, rows, :].astype(F32), *gains)
        )
    joined, quarter = stacked_pair(*zip(*pairs))
    turned = joined.T
    for part, right in enumerate((joined, quarter)):
        for chunk in range(2):
            cols = pl.ds(chunk * 256, 256)
            model = dot(turned[chunk * 256 : (chunk + 1) * 256], right, NN_DIMS)
            residual[part, cols, :] = (observed[part, cols, :].astype(F32) - model).astype(BF16)
            copies.append(
                pltpu.make_async_copy(
                    residual.at[part, cols],
                    residual_hbm.at[part, cols],
                    sent.at[2 * chunk + part],
                )
            )
            copies[-1].start()
    for copy in copies:
        copy.wait()


def peel(observed, beams, smooth):
    vmem = pl.BlockSpec(memory_space=pltpu.VMEM)
    return pl.pallas_call(
        peel_kernel,
        out_shape=(
            jax.ShapeDtypeStruct((2, S, S), BF16),
            jax.ShapeDtypeStruct((2, 2, S), F32),
        ),
        in_specs=[vmem, vmem, vmem],
        out_specs=(pl.BlockSpec(memory_space=pltpu.HBM),) * 2,
        scratch_shapes=[
            pltpu.VMEM((2, S, S), BF16),
            pltpu.VMEM((2, 2, S), F32),
            pltpu.SemaphoreType.DMA((5,)),
        ],
        compiler_params=pltpu.CompilerParams(vmem_limit_bytes=20 * 2**20),
        cost_estimate=pl.CostEstimate(flops=10**9, bytes_accessed=3 * 10**6, transcendentals=0),
        name="peel",
    )(observed, beams, smooth)


def local(observed, source_beams, source_order, initial_gains, blending):
    freqs, times = lax.axis_size("freq"), lax.axis_size("tm")
    observed_block = observed[0, 0]
    sums, beams, rows = terms(
        observed_block,
        source_beams[0, 0],
        source_order.reshape(2, HALF),
        initial_gains[0],
        blending,
    )
    pieces = lax.all_to_all(sums, "tm", split_axis=0, concat_axis=0, tiled=True)
    totals = jnp.sum(pieces, axis=0).reshape(3, 8, LANES)
    damped = 0.5 * (totals[:2] / totals[2])
    sent = jnp.broadcast_to(damped[None, :, None], (freqs // TEAM, 2, 2, 8, LANES))
    bands = lax.all_to_all(
        sent.reshape(freqs, 8, LANES), "freq", split_axis=0, concat_axis=0, tiled=True
    )
    mixed = jnp.sum(rows[:, :, None, None] * bands[None], axis=1)
    spread = jnp.broadcast_to(mixed[:, None], (2, times, 8, LANES))
    groups = [
        [(team * TEAM + side * 2 + core) * times + time for side in range(2) for time in range(times)]
        for team in range(freqs // TEAM)
        for core in range(2)
    ]
    smooth = lax.all_to_all(
        spread.reshape(2 * times, 8, LANES),
        ("freq", "tm"),
        split_axis=0,
        concat_axis=0,
        tiled=True,
        axis_index_groups=groups,
    )
    residual, gains_out = peel(observed_block, beams, smooth)
    return (residual[None, None], gains_out[None])


def solution(mesh):
    return jax.shard_map(
        local,
        mesh=mesh,
        in_specs=(
            P("freq", "tm", None, None, None),
            P("freq", "tm", None, None, None),
            P(),
            P("freq", None, None, None),
            P(),
        ),
        out_specs=(P("freq", "tm", None, None, None), P("freq", None, "tm", None)),
        check_vma=False,
    )
```

```python
import jax
import jax.numpy as jnp
from jax import lax
from jax.experimental import pallas as pl
from jax.experimental.pallas import tpu as pltpu
from jax.sharding import PartitionSpec as P

S = 512
K = 32
P_SIZE = 8
N = K * P_SIZE
HALF = 128
GROUP = 16
LANES = 128
TEAM = 4
FIRST_TIME = 12
FIRST_BAND = 28
NT_DIMS = (((1,), (1,)), ((), ()))
NN_DIMS = (((1,), (0,)), ((), ()))
F32 = jnp.float32
BF16 = jnp.bfloat16


def dot(left, right, dims):
    return lax.dot_general(left, right, dims, preferred_element_type=F32)


def rotated_pair(real, imag, gains_real, gains_imag):
    return gains_real * real - gains_imag * imag, gains_real * imag + gains_imag * real


def repeat_rows(rows):
    return jnp.concatenate([rows] * P_SIZE, axis=0)


def direction_sums(values):
    total = values[:GROUP]
    for at in range(1, P_SIZE):
        total = total + values[at * GROUP : (at + 1) * GROUP]
    return total


def store_pair(wide, half, lanes, real, imag):
    base = half * 2 * HALF
    low, size = lanes
    real, imag = real.astype(BF16), imag.astype(BF16)
    wide[pl.ds(base, HALF), pl.ds(low, size)] = real
    wide[pl.ds(base + HALF, HALF), pl.ds(low, size)] = imag
    wide[pl.ds(base, HALF), pl.ds(S + low, size)] = -imag
    wide[pl.ds(base + HALF, HALF), pl.ds(S + low, size)] = real


def stacked_pair(reals, imags):
    joined, quarter = [], []
    for real, imag in zip(reals, imags):
        real, imag = real.astype(BF16), imag.astype(BF16)
        joined += [real, imag]
        quarter += [-imag, real]
    return jnp.concatenate(joined, axis=0), jnp.concatenate(quarter, axis=0)


def terms_kernel(
    observed_hbm, catalogue_hbm, order_hbm, gains_hbm, blending_hbm, sums, beams, rows_out,
    observed, catalogue, order, gains, blending, exact, wide, turned, misfit, arrived,
):
    copies = [
        pltpu.make_async_copy(source, target, arrived.at[at])
        for at, (source, target) in enumerate(
            (
                (order_hbm, order),
                (catalogue_hbm, catalogue),
                (gains_hbm, gains),
                (observed_hbm, observed),
                (blending_hbm, blending),
            )
        )
    ]
    for copy in copies:
        copy.start()
    copies[0].wait()
    lane = lax.broadcasted_iota(jnp.int32, (2, HALF), 1)
    listed = jnp.take_along_axis(order[...], (lane % GROUP) * P_SIZE + lane // GROUP, axis=1)
    listed = jnp.concatenate([listed[0:1], listed[1:2]], axis=1)
    source = lax.broadcasted_iota(jnp.int32, (N, N), 0)
    pick = jnp.where(source == listed, 1.0, 0.0).astype(BF16).T
    copies[1].wait()
    for part in range(2):
        picked = dot(pick, catalogue[part], NN_DIMS)
        exact[part] = picked
        beams[part] = picked.astype(BF16)
    copies[2].wait()
    copies[3].wait()
    copies[4].wait()
    freq = lax.axis_index("freq")
    first = freq - 2 * ((freq // 2) % 2)
    mixing = jnp.concatenate([blending[pl.ds(first, 1), :], blending[pl.ds(first + 2, 1), :]], axis=0)
    rows_out[...] = jnp.concatenate([mixing[:, FIRST_BAND:], mixing[:, :FIRST_BAND]], axis=1)
    for half in range(2):
        rows = pl.ds(half * HALF, HALF)
        ks = pl.ds(half * GROUP, GROUP)
        real, imag = rotated_pair(
            exact[0, rows, :],
            exact[1, rows, :],
            repeat_rows(gains[0, ks, :]),
            repeat_rows(gains[1, ks, :]),
        )
        store_pair(wide, half, (0, S), real, imag)
    turned[...] = wide[:, :S].T
    for part in range(2):
        cols = pl.ds(part * S, S)
        model = dot(turned[...], wide[:, cols], NN_DIMS)
        misfit[:, cols] = (observed[part].astype(F32) - model).astype(BF16)
    everything = dot(wide[...], misfit[...], NT_DIMS)
    row_dir = lax.broadcasted_iota(jnp.int32, (HALF, HALF), 0) % GROUP
    col_dir = lax.broadcasted_iota(jnp.int32, (HALF, HALF), 1) % GROUP
    same = row_dir == col_dir
    weights = []
    for half in range(2):
        rows = pl.ds(half * HALF, HALF)
        block = wide[pl.ds(half * 2 * HALF, 2 * HALF), :S]
        grid = dot(block, block, NT_DIMS)
        gram_real = jnp.where(same, grid[:HALF, :HALF] + grid[HALF:, HALF:], 0.0)
        gram_imag = jnp.where(same, grid[:HALF, HALF:] - grid[HALF:, :HALF], 0.0)
        high_real, high_imag = gram_real.astype(BF16), gram_imag.astype(BF16)
        low_real = (gram_real - high_real.astype(F32)).astype(BF16)
        low_imag = (gram_imag - high_imag.astype(F32)).astype(BF16)
        gram = jnp.concatenate(
            [
                jnp.concatenate([high_real, high_imag, low_real, low_imag], axis=1),
                jnp.concatenate([high_imag, -high_real, low_imag, -low_real], axis=1),
            ],
            axis=0,
        )
        both = jnp.concatenate([beams[0, rows, :], beams[1, rows, :]] * 2, axis=0)
        inner = dot(gram, both, NN_DIMS)
        weights.append(
            direction_sums(exact[0, rows, :] * inner[:HALF] - exact[1, rows, :] * inner[HALF:])
        )
    for half in range(2):
        rows = pl.ds(half * HALF, HALF)
        ks = pl.ds(half * GROUP, GROUP)
        product = everything[half * 2 * HALF : (half + 1) * 2 * HALF]
        real, imag = exact[0, rows, :], exact[1, rows, :]
        weight = weights[half]
        pull_real = direction_sums(real * product[:HALF] + imag * product[HALF:])
        pull_imag = direction_sums(real * product[HALF:] - imag * product[:HALF])
        values = (
            pull_real + 2.0 * gains[0, ks, :] * weight,
            pull_imag + 2.0 * gains[1, ks, :] * weight,
            weight,
        )
        for group in range(2):
            for block in range(4):
                piece = ((half * 2 + group) * 4 + block - FIRST_TIME) % 16
                for part, value in enumerate(values):
                    sums[piece, pl.ds(part * 8, 8), :] = value[
                        group * 8 : group * 8 + 8, block * LANES : (block + 1) * LANES
                    ]


def terms(*operands):
    bands = operands[4].shape[0]
    return pl.pallas_call(
        terms_kernel,
        out_shape=(
            jax.ShapeDtypeStruct((16, 24, LANES), F32),
            jax.ShapeDtypeStruct((2, N, S), BF16),
            jax.ShapeDtypeStruct((2, bands), F32),
        ),
        in_specs=[pl.BlockSpec(memory_space=pltpu.HBM)] * 5,
        out_specs=(pl.BlockSpec(memory_space=pltpu.VMEM),) * 3,
        scratch_shapes=[
            pltpu.VMEM((2, S, S), BF16),
            pltpu.VMEM((2, N, S), BF16),
            pltpu.VMEM((2, HALF), jnp.int32),
            pltpu.VMEM((2, K, S), F32),
            pltpu.VMEM((bands, bands), F32),
            pltpu.VMEM((2, N, S), F32),
            pltpu.VMEM((2 * N, 2 * S), BF16),
            pltpu.VMEM((S, 2 * N), BF16),
            pltpu.VMEM((S, 2 * S), BF16),
            pltpu.SemaphoreType.DMA((5,)),
        ],
        compiler_params=pltpu.CompilerParams(vmem_limit_bytes=20 * 2**20),
        cost_estimate=pl.CostEstimate(flops=2 * 10**9, bytes_accessed=2 * 10**6, transcendentals=0),
        name="terms",
    )(*[pltpu.with_memory_space_constraint(operand, pltpu.HBM) for operand in operands])


def gathered(part, time):
    return part * 16 + (time + 16 - FIRST_TIME) % 16


def peel_kernel(observed, beams, smooth, residual_hbm, gains_hbm, residual, gains_out, sent):
    slot = lax.axis_index("tm")
    group = slot // 4
    row = (slot % 4) * 2
    for part in range(2):
        for block in range(4):
            gains_out[part, :, pl.ds(block * LANES, LANES)] = smooth[
                gathered(part, group * 4 + block), pl.ds(row, 2), :
            ]
    copies = [pltpu.make_async_copy(gains_out, gains_hbm, sent.at[4])]
    copies[0].start()
    pairs = []
    for half in range(2):
        rows = pl.ds(half * HALF, HALF)
        gains = [
            repeat_rows(
                jnp.concatenate(
                    [
                        jnp.concatenate(
                            [smooth[gathered(part, (2 * half + group) * 4 + block)] for block in range(4)],
                            axis=1,
                        )
                        for group in range(2)
                    ],
                    axis=0,
                )
            )
            for part in range(2)
        ]
        pairs.append(
            rotated_pair(beams[0, rows, :].astype(F32), beams[1, rows, :].astype(F32), *gains)
        )
    joined, quarter = stacked_pair(*zip(*pairs))
    turned = joined.T
    for part, right in enumerate((joined, quarter)):
        for chunk in range(2):
            cols = pl.ds(chunk * 256, 256)
            model = dot(turned[chunk * 256 : (chunk + 1) * 256], right, NN_DIMS)
            residual[part, cols, :] = (observed[part, cols, :].astype(F32) - model).astype(BF16)
            copies.append(
                pltpu.make_async_copy(
                    residual.at[part, cols],
                    residual_hbm.at[part, cols],
                    sent.at[2 * chunk + part],
                )
            )
            copies[-1].start()
    for copy in copies:
        copy.wait()


def peel(observed, beams, smooth):
    vmem = pl.BlockSpec(memory_space=pltpu.VMEM)
    return pl.pallas_call(
        peel_kernel,
        out_shape=(
            jax.ShapeDtypeStruct((2, S, S), BF16),
            jax.ShapeDtypeStruct((2, 2, S), F32),
        ),
        in_specs=[vmem, vmem, vmem],
        out_specs=(pl.BlockSpec(memory_space=pltpu.HBM),) * 2,
        scratch_shapes=[
            pltpu.VMEM((2, S, S), BF16),
            pltpu.VMEM((2, 2, S), F32),
            pltpu.SemaphoreType.DMA((5,)),
        ],
        compiler_params=pltpu.CompilerParams(vmem_limit_bytes=20 * 2**20),
        cost_estimate=pl.CostEstimate(flops=10**9, bytes_accessed=3 * 10**6, transcendentals=0),
        name="peel",
    )(observed, beams, smooth)


def local(observed, source_beams, source_order, initial_gains, blending):
    freqs, times = lax.axis_size("freq"), lax.axis_size("tm")
    observed_block = observed[0, 0]
    sums, beams, rows = terms(
        observed_block,
        source_beams[0, 0],
        source_order.reshape(2, HALF),
        initial_gains[0],
        blending,
    )
    order = [
        [freq * times + (at + FIRST_TIME) % times for at in range(times)] for freq in range(freqs)
    ]
    pieces = lax.all_to_all(
        sums, ("freq", "tm"), split_axis=0, concat_axis=0, tiled=True, axis_index_groups=order
    )
    totals = jnp.sum(pieces, axis=0).reshape(3, 8, LANES)
    damped = 0.5 * (totals[:2] / totals[2])
    sent = jnp.broadcast_to(damped[None, :, None], (freqs // TEAM, 2, 2, 8, LANES))
    bands = lax.all_to_all(
        sent.reshape(freqs, 8, LANES),
        "freq",
        split_axis=0,
        concat_axis=0,
        tiled=True,
        axis_index_groups=[[(at + FIRST_BAND) % freqs for at in range(freqs)]],
    )
    mixed = jnp.sum(rows[:, :, None, None] * bands[None], axis=1)
    spread = jnp.broadcast_to(mixed[:, None], (2, times, 8, LANES))
    groups = [
        [
            (team * TEAM + side * 2 + core) * times + (at + FIRST_TIME) % times
            for side in range(2)
            for at in range(times)
        ]
        for team in range(freqs // TEAM)
        for core in range(2)
    ]
    smooth = lax.all_to_all(
        spread.reshape(2 * times, 8, LANES),
        ("freq", "tm"),
        split_axis=0,
        concat_axis=0,
        tiled=True,
        axis_index_groups=groups,
    )
    residual, gains_out = peel(observed_block, beams, smooth)
    return (residual[None, None], gains_out[None])


def solution(mesh):
    return jax.shard_map(
        local,
        mesh=mesh,
        in_specs=(
            P("freq", "tm", None, None, None),
            P("freq", "tm", None, None, None),
            P(),
            P("freq", None, None, None),
            P(),
        ),
        out_specs=(P("freq", "tm", None, None, None), P("freq", None, "tm", None)),
        check_vma=False,
    )
```
